32 devices in a mesh: row: 8 (over z, x), col: 4 (over y, core).
Axes of the slice: x: 2, y: 2, z: 4, core: 2. Of those that a mesh axis runs over, the one named last changes fastest.
Arguments:
- mom_a: float32 [1536, 12288], P('row', 'col'), may hold values from -6 to 6
- grad_a: float32 [1536, 12288], P('row', 'col'), may hold values from -6 to 6
- basis_a: float32 [512, 12288], P('row', 'col'), may hold values from -0.0546875 to 0.0546875
- mom_b: float32 [7168, 1536], P('row', 'col'), may hold values from -6 to 6
- grad_b: float32 [7168, 1536], P('row', 'col'), may hold values from -6 to 6
- basis_b: float32 [512, 1536], P('row', 'col'), may hold values from -0.15625 to 0.15625
Outputs:
- new_mom_a: float32 [1536, 12288], P('row', 'col')
- update_a: bfloat16 [1536, 12288], P('row', 'col')
- new_basis_a: float32 [512, 12288], P('row', 'col')
- new_mom_b: float32 [7168, 1536], P('row', 'col')
- update_b: bfloat16 [7168, 1536], P('row', 'col')
- new_basis_b: float32 [512, 1536], P('row', 'col')
The draws below stay inside these ranges and needn't reach their ends.
All inputs are finite; a program needn't handle non-finite values.
Results may differ from the reference program's by a relative error of at most 0.0049.
Values sent between devices are 32-bit elements; how exact they have to be, the bound alone decides.
A program may use at most 128 MiB of HBM per device.

```python
import math
import jax
import jax.numpy as jnp
from jax import lax

M_A = 1536
N_A = 12288
M_B = 7168
N_B = 1536
RANK = 512


def strong_factors(key, offset, row_count, col_count):
    strong_rank = 3 * RANK // 4
    left_factor = jax.random.normal(jax.random.fold_in(key, offset + 1), (row_count, strong_rank), jnp.float32) / math.sqrt(row_count)
    right_factor = jax.random.normal(jax.random.fold_in(key, offset + 2), (strong_rank, col_count), jnp.float32) / math.sqrt(col_count)
    low_end = 1.0
    high_end = 5.0
    strength = jnp.exp(jax.random.uniform(jax.random.fold_in(key, offset + 3), (strong_rank,), jnp.float32, math.log(low_end), math.log(high_end)))
    ratios = jax.random.uniform(jax.random.fold_in(key, offset + 4), (strong_rank,), jnp.float32, 0.5, 1.5)
    amplitude = 0.2 * math.sqrt(row_count * col_count / RANK)
    return (left_factor * amplitude, right_factor, strength, ratios)


def noise_field(key, offset, row_count, col_count):
    noise_term = jax.random.normal(key_mix(key, offset), (row_count, col_count), jnp.float32)
    return 0.2 * noise_term


def key_mix(key, offset):
    return jax.random.fold_in(key, offset)


def draw_matrix(key, offset, row_count, col_count, second):
    left_factor, right_factor, strength, ratios = strong_factors(key, offset, row_count, col_count)
    if second:
        weights = strength * ratios
        noise_offset = offset + 20
    else:
        weights = strength
        noise_offset = offset + 10
    low_rank = jnp.dot(left_factor * weights[None, :], right_factor, precision=lax.Precision.HIGHEST, preferred_element_type=jnp.float32)
    noise_term = noise_field(key, noise_offset, row_count, col_count)
    return jnp.clip(low_rank + noise_term, -6.0, 6.0)


def draw_mom_a(key, part):
    return draw_matrix(key, 100, M_A, N_A, False)


def draw_grad_a(key, part):
    return draw_matrix(key, 100, M_A, N_A, True)


def draw_mom_b(key, part):
    return draw_matrix(key, 200, M_B, N_B, False)


def draw_grad_b(key, part):
    return draw_matrix(key, 200, M_B, N_B, True)


def levels(stream_key, shape, pieces, low, largest):
    def one(position, blocks):
        heights = jax.random.uniform(jax.random.fold_in(jax.random.fold_in(stream_key, 6), position), (blocks,), jnp.float32, low / len(pieces), largest / len(pieces))
        return jnp.repeat(jnp.exp(heights), shape[position] // blocks).reshape((-1,) + (1,) * (len(shape) - position - 1))

    factor_of = one(*pieces[0])
    for cut in pieces[1:]:
        factor_of = factor_of * one(*cut)
    return factor_of


def bell_draw(rng, dims, width, limit, split=(), held_as=jnp.bfloat16):
    values = jax.random.normal(rng, dims, jnp.float32) * width
    if len(split) > 0:
        values = levels(rng, dims, split, -0.22, 0.18) * values
    return jnp.clip(values, min=-limit, max=limit).astype(held_as)


def setup_inputs(seed: int = 0) -> dict:
    keys = jax.random.split(jax.random.key(seed), 7)
    return {
        "mom_a": draw_mom_a(jax.random.fold_in(keys[6], 71), 0),
        "grad_a": draw_grad_a(jax.random.fold_in(keys[6], 71), 0),
        "basis_a": bell_draw(keys[2], (RANK, N_A), N_A ** -0.5, 0.0546875, ((0, 8), (1, 4)), jnp.float32),
        "mom_b": draw_mom_b(jax.random.fold_in(keys[6], 71), 0),
        "grad_b": draw_grad_b(jax.random.fold_in(keys[6], 71), 0),
        "basis_b": bell_draw(keys[5], (RANK, N_B), N_B ** -0.5, 0.15625, ((0, 8), (1, 4)), jnp.float32),
    }


MU = 0.95
EPS = 1e-06

def dion_step(mom, grad, basis):
    highest = lax.Precision.HIGHEST
    buffer = MU * mom + grad
    proj = jnp.dot(buffer.astype(jnp.float32), basis.T.astype(jnp.float32), precision=highest, preferred_element_type=jnp.float32)
    gram = jnp.dot(proj.T.astype(jnp.float32), proj.astype(jnp.float32), precision=highest, preferred_element_type=jnp.float32)
    lower = jnp.linalg.cholesky(gram)
    ortho = lax.linalg.triangular_solve(lower, proj, left_side=False, lower=True, transpose_a=True)
    trans = jnp.dot(ortho.T.astype(jnp.float32), buffer.astype(jnp.float32), precision=highest, preferred_element_type=jnp.float32)
    new_mom = buffer - (1.0 - MU) * jnp.dot(ortho.astype(jnp.float32), trans.astype(jnp.float32), precision=highest, preferred_element_type=jnp.float32)
    norms = jnp.sqrt(lax.optimization_barrier(jnp.sum(trans * trans, axis=1, keepdims=True)) + EPS)
    new_basis = trans / norms
    scale = math.sqrt(buffer.shape[0] * buffer.shape[1] / basis.shape[0])
    update = (jnp.dot(ortho.astype(jnp.float32), new_basis.astype(jnp.float32), precision=highest, preferred_element_type=jnp.float32) * scale).astype(jnp.bfloat16)
    return (new_mom, update, new_basis)

def reference(mom_a, grad_a, basis_a, mom_b, grad_b, basis_b):
    first = dion_step(mom_a, grad_a, basis_a)
    second = dion_step(mom_b, grad_b, basis_b)
    return (first[0], first[1], first[2], second[0], second[1], second[2])
```

```python
import functools
import math

import jax
import jax.numpy as jnp
from jax import lax
from jax.experimental import pallas as pl
from jax.experimental.pallas import tpu as pltpu
from jax.sharding import PartitionSpec as P

MU = 0.95
EPS = 1e-06
BLOCK = 128
HIGHEST = lax.Precision.HIGHEST


def dot(x, y, contract=((1,), (0,))):
    return lax.dot_general(
        x, y, (contract, ((), ())), precision=HIGHEST, preferred_element_type=jnp.float32
    )


def inverse_kernel(rank, *refs):
    count = len(refs) // 4
    grams, outs = refs[:count], refs[count : 2 * count]
    works, diags = refs[2 * count : 3 * count], refs[3 * count :]
    eye_rows = lax.broadcasted_iota(jnp.int32, (rank, rank), 0)
    eye_cols = lax.broadcasted_iota(jnp.int32, (rank, rank), 1)
    for gram, work in zip(grams, works):
        work[:, :rank] = gram[...]
        work[:, rank:] = (eye_rows == eye_cols).astype(jnp.float32)
    rows = lax.broadcasted_iota(jnp.int32, (BLOCK, 1), 0)
    lanes = lax.broadcasted_iota(jnp.int32, (1, BLOCK), 1)
    for k in range(rank // BLOCK):
        low, high = k * BLOCK, (k + 1) * BLOCK
        for work, diag in zip(works, diags):
            diag[:, :BLOCK] = work[low:high, low:high]
            diag[:, BLOCK:] = (rows == lanes).astype(jnp.float32)

        def step(j, carry):
            for diag in diags:
                here = lanes == j
                row = diag[pl.ds(j, 1), :]
                col = jnp.sum(jnp.where(here, diag[:, :BLOCK], 0.0), axis=1, keepdims=True)
                pivot = jnp.sum(jnp.where(here, row[:, :BLOCK], 0.0), axis=1, keepdims=True)
                factor = jnp.where(rows > j, col * (1.0 / pivot), 0.0)
                diag[...] = diag[...] - factor * row
            return carry

        lax.fori_loop(0, BLOCK, step, 0)
        width = slice(low, rank + high)
        for work, diag in zip(works, diags):
            pivots = jnp.sum(
                jnp.where(rows == lanes, diag[:, :BLOCK], 0.0), axis=1, keepdims=True
            )
            inverse = diag[:, BLOCK:] * (1.0 / jnp.sqrt(pivots))
            panel = dot(inverse, work[low:high, width])
            work[low:high, width] = panel
            if high < rank:
                factors = panel[:, BLOCK : rank - low]
                work[high:, width] = work[high:, width] - dot(factors, panel, ((0,), (0,)))
    for work, out in zip(works, outs):
        out[...] = work[:, rank:]


def inverse_factors(*grams):
    rank = grams[0].shape[0]
    count = len(grams)
    return pl.pallas_call(
        functools.partial(inverse_kernel, rank),
        out_shape=[jax.ShapeDtypeStruct((rank, rank), jnp.float32)] * count,
        in_specs=[pl.BlockSpec(memory_space=pltpu.VMEM)] * count,
        out_specs=[pl.BlockSpec(memory_space=pltpu.VMEM)] * count,
        scratch_shapes=[pltpu.VMEM((rank, 2 * rank), jnp.float32)] * count
        + [pltpu.VMEM((BLOCK, 2 * BLOCK), jnp.float32)] * count,
        compiler_params=pltpu.CompilerParams(vmem_limit_bytes=24 * 1024 * 1024),
    )(*grams)


def reduce_rows(partial_sum):
    share_count = lax.axis_size("row")
    shares = partial_sum.reshape(share_count, -1, partial_sum.shape[1])
    return jnp.sum(lax.all_to_all(shares, "row", 0, 0), axis=0)


def shards(mom_a, grad_a, basis_a, mom_b, grad_b, basis_b):
    row_count, col_count = lax.axis_size("row"), lax.axis_size("col")
    buffer_a, buffer_b = MU * mom_a + grad_a, MU * mom_b + grad_b
    last = ((1,), (1,))
    first = ((0,), (0,))
    both = lax.all_gather(jnp.concatenate([basis_a, basis_b], axis=1), "row", axis=0, tiled=True)
    full_a, full_b = both[:, : buffer_a.shape[1]], both[:, buffer_a.shape[1] :]
    partial_a, partial_b, held_a = lax.optimization_barrier(
        (dot(buffer_a, full_a, last), dot(buffer_b, full_b, last), buffer_a)
    )
    proj_a, proj_b = lax.psum((partial_a, partial_b), "col")
    tall_a = lax.all_to_all(held_a, "row", 1, 0, tiled=True)
    proj_a, proj_b, tall_a = lax.optimization_barrier((proj_a, proj_b, tall_a))
    rank = proj_a.shape[1]
    share = rank // row_count

    shares_b = reduce_rows(
        jnp.concatenate([dot(proj_b, proj_b, first), dot(proj_b, buffer_b, first)], axis=1)
    )
    share_b = shares_b[:, rank:]
    gathered = lax.all_gather(jnp.concatenate([proj_a, shares_b[:, :rank]]), "row", axis=0)
    proj_rows = proj_a.shape[0]
    all_a = gathered[:, :proj_rows].reshape(-1, rank)
    gram_b = gathered[:, proj_rows:].reshape(rank, rank)
    gram_a = dot(all_a, all_a, first)
    block_a = dot(all_a, tall_a, first)
    inverse_a, inverse_b = inverse_factors(gram_a, gram_b)

    width_a, width_b = block_a.shape[1], share_b.shape[1]
    width = max(width_a, width_b)
    products = lax.all_gather(
        jnp.concatenate(
            [
                jnp.pad(block_a, ((0, 0), (0, width - width_a))),
                jnp.pad(share_b, ((0, 0), (0, width - width_b))),
            ]
        ),
        "row",
        axis=1,
        tiled=True,
    )
    product_a = products[:rank]
    product_b = products[rank:].reshape(share, row_count, width).swapaxes(0, 1)
    product_b = product_b.reshape(rank, width)[:, :width_b]
    if width != width_a:
        product_a = product_a.reshape(rank, row_count, width)[:, :, :width_a].reshape(rank, -1)

    ortho_a, ortho_b = dot(proj_a, inverse_a, last), dot(proj_b, inverse_b, last)
    trans_a, trans_b = dot(inverse_a, product_a), dot(inverse_b, product_b)
    squares_a, squares_b = lax.psum(
        (
            jnp.sum(trans_a * trans_a, axis=1, keepdims=True),
            jnp.sum(trans_b * trans_b, axis=1, keepdims=True),
        ),
        "col",
    )
    start = lax.axis_index("row") * share
    first_out = finish(buffer_a, ortho_a, trans_a, squares_a, start, share)
    second_out = finish(buffer_b, ortho_b, trans_b, squares_b, start, share)
    return (*first_out, *second_out)


def finish(buffer, ortho, trans, squares, start, share):
    rank = ortho.shape[1]
    total_rows = buffer.shape[0] * lax.axis_size("row")
    total_cols = buffer.shape[1] * lax.axis_size("col")
    full_basis = trans / jnp.sqrt(squares + EPS)
    own_basis = lax.dynamic_slice_in_dim(full_basis, start, share, 0)
    new_mom = buffer - (1.0 - MU) * dot(ortho, trans)
    update = dot(ortho, full_basis) * math.sqrt(total_rows * total_cols / rank)
    return new_mom, update.astype(jnp.bfloat16), own_basis


def solution(mesh):
    spec = P("row", "col")
    return jax.shard_map(
        shards, mesh=mesh, in_specs=(spec,) * 6, out_specs=(spec,) * 6, check_vma=False
    )
```
